512 devices in a mesh: grp: 4 (over x), dev: 128 (over z, y, core).
Axes of the slice: x: 4, y: 8, z: 8, core: 2. Of those that a mesh axis runs over, the one named last changes fastest.
Arguments:
- blocks: bfloat16 [4096, 64, 4096], P(('grp', 'dev')), may hold values from -6 to 6
- coords: int32 [3, 4096], P(None, ('grp', 'dev')), may hold values from 0 to 255, as said below
- counts: int32 [512], P(('grp', 'dev')), may hold values from 1 to 8, as said below
- row_place: int32 [256], replicated, may hold values from 0 to 255, as said below
- factor_one: bfloat16 [256, 4096], P('dev'), may hold values from -0.75 to 0.75
- factor_two: bfloat16 [256, 4096], P('dev'), may hold values from -0.75 to 0.75
- factor_three: bfloat16 [256, 4096], P('dev'), may hold values from -0.75 to 0.75
Outputs:
- new_rows: float32 [256, 4096], P('dev')
- gram: float32 [64, 64], replicated
The draws below stay inside these ranges and needn't reach their ends.
Inputs may be any that keep to these rules, and one draw needn't show every extreme that they name: `coords`: every mode-1 id of a slot on the device with dev index d has its row-block position in [d * 2, (d + 1) * 2); on one device, the row-block positions of the mode-2 ids of its 8 slots lie in pairwise different ranges [e * 2, (e + 1) * 2), and so do those of the mode-3 ids. `counts`: some device has all 8 slots live. `row_place`: A permutation of 0 to 255.
All inputs are finite; a program needn't handle non-finite values.
Results may differ from the reference program's by a relative error of at most 0.0056.
Values may be sent and summed in bfloat16 or wider, within the bound.
A program may use at most 128 MiB of HBM per device.

```python
import jax
import jax.numpy as jnp
from jax import lax

BLOCK_EDGE = 64
R = 64
DEVICE_BLOCKS = 8
DEVICE_ROW_BLOCKS = 2
NRB = 256
TOTAL_SLOTS = 4096
N_GRP = 4
N_DEV = 128


def shared_place(key):
    return jax.random.permutation(jax.random.fold_in(key, 7), NRB).astype(jnp.int32)


def draw_row_place(key, part):
    return shared_place(key)


def distinct_owners(key):
    total = N_GRP * N_DEV
    scores = jax.random.randint(key, (total, N_DEV), 0, 4096).astype(jnp.int32)
    scores = scores * N_DEV + jnp.arange(N_DEV).astype(jnp.int32)[None, :]
    sort_order = jnp.argsort(scores, axis=1, stable=True).astype(jnp.int32)
    return sort_order[:, :DEVICE_BLOCKS].reshape(TOTAL_SLOTS)


def draw_coords(key, part):
    place = shared_place(key)
    id_at = jnp.argsort(place).astype(jnp.int32)
    block_index = jnp.arange(TOTAL_SLOTS).astype(jnp.int32)
    dev_index = block_index // DEVICE_BLOCKS % N_DEV
    local_part = jax.random.randint(jax.random.fold_in(key, 11), (TOTAL_SLOTS,), 0, DEVICE_ROW_BLOCKS).astype(jnp.int32)
    ids_one = id_at[dev_index * DEVICE_ROW_BLOCKS + local_part]
    owner_two = distinct_owners(jax.random.fold_in(key, 13))
    owner_three = distinct_owners(jax.random.fold_in(key, 17))
    local_part_two = jax.random.randint(jax.random.fold_in(key, 29), (TOTAL_SLOTS,), 0, DEVICE_ROW_BLOCKS).astype(jnp.int32)
    local_part_three = jax.random.randint(jax.random.fold_in(key, 31), (TOTAL_SLOTS,), 0, DEVICE_ROW_BLOCKS).astype(jnp.int32)
    ids_two = id_at[owner_two * DEVICE_ROW_BLOCKS + local_part_two]
    ids_three = id_at[owner_three * DEVICE_ROW_BLOCKS + local_part_three]
    return jnp.stack([ids_one, ids_two, ids_three], axis=0).astype(jnp.int32)


def draw_counts(key, part):
    total = N_GRP * N_DEV
    values = jax.random.randint(jax.random.fold_in(key, 19), (total,), 1, DEVICE_BLOCKS + 1).astype(jnp.int32)
    fullest = jax.random.randint(jax.random.fold_in(key, 23), (), 0, total)
    return values.at[fullest].set(DEVICE_BLOCKS).astype(jnp.int32)


def level_of(rng, extent, pieces, low, high):
    level, own = 1.0, jax.random.fold_in(rng, 6)
    for axis_at, shards_of in pieces:
        steps = jnp.exp(jax.random.uniform(jax.random.fold_in(own, axis_at), (shards_of,), jnp.float32, low / len(pieces), high / len(pieces)))
        level = level * jnp.repeat(steps, extent[axis_at] // shards_of).reshape([-1 if axis == axis_at else 1 for axis in range(len(extent))])
    return level


def gaussian(rng, dims, spread, limit, split=(), kind=jnp.bfloat16):
    result = spread * jax.random.normal(rng, dims, jnp.float32)
    if split:
        result = result * level_of(rng, dims, split, -0.22, 0.18)
    return jnp.clip(result, -limit, limit).astype(kind)


def setup_inputs(seed: int = 0) -> dict:
    seeds = jax.random.split(jax.random.key(seed), 8)
    return {
        "blocks": gaussian(seeds[0], (TOTAL_SLOTS, BLOCK_EDGE, BLOCK_EDGE * BLOCK_EDGE), 1.0, 6.0, ((0, 512),)),
        "coords": draw_coords(jax.random.fold_in(seeds[7], 71), 0),
        "counts": draw_counts(jax.random.fold_in(seeds[7], 71), 0),
        "row_place": draw_row_place(jax.random.fold_in(seeds[7], 71), 0),
        "factor_one": gaussian(seeds[4], (NRB, BLOCK_EDGE * R), BLOCK_EDGE ** -0.5, 0.75, ((0, 128),)),
        "factor_two": gaussian(seeds[5], (NRB, BLOCK_EDGE * R), BLOCK_EDGE ** -0.5, 0.75, ((0, 128),)),
        "factor_three": gaussian(seeds[6], (NRB, BLOCK_EDGE * R), BLOCK_EDGE ** -0.5, 0.75, ((0, 128),)),
    }


def reference(blocks, coords, counts, row_place, factor_one, factor_two, factor_three):
    slots = blocks.shape[0]
    block_index = jnp.arange(slots).astype(jnp.int32)
    owner = (block_index // DEVICE_BLOCKS).astype(jnp.int32)
    alive = (block_index % DEVICE_BLOCKS < counts[owner]).astype(jnp.float32)
    places = row_place[coords].astype(jnp.int32)

    def advance(panels, item):
        block, p_i, p_j, p_k, live = item
        upper = factor_two[p_j].reshape(BLOCK_EDGE, R)
        lower = factor_three[p_k].reshape(BLOCK_EDGE, R)
        first = jnp.dot(block.reshape(BLOCK_EDGE * BLOCK_EDGE, BLOCK_EDGE), lower, preferred_element_type=jnp.float32).astype(jnp.bfloat16)
        first = first.reshape(BLOCK_EDGE, BLOCK_EDGE, R).astype(jnp.float32)
        second = jnp.einsum('ajs,jr->ars', first, upper.astype(jnp.float32))
        contrib = second.reshape(BLOCK_EDGE, R * R) * live
        start = (p_i * BLOCK_EDGE).astype(jnp.int32)
        older = lax.dynamic_slice_in_dim(panels, start, BLOCK_EDGE, 0)
        panels = lax.dynamic_update_slice_in_dim(panels, older + contrib, start, 0)
        return (panels, None)
    panels0 = jnp.zeros((NRB * BLOCK_EDGE, R * R), jnp.float32)
    panels, _ = lax.scan(advance, panels0, (blocks, places[0], places[1], places[2], alive))
    panel_b = panels.astype(jnp.bfloat16)
    old_rows = factor_one.reshape(NRB * BLOCK_EDGE, R)
    proj = jnp.dot(panel_b.T, old_rows, preferred_element_type=jnp.float32).astype(jnp.bfloat16)
    rows = jnp.dot(panel_b, proj, preferred_element_type=jnp.float32)
    gmat = jnp.dot(rows.T, rows, precision=lax.Precision.HIGHEST, preferred_element_type=jnp.float32)
    trace_value = jnp.trace(gmat)
    new_rows = (rows * lax.rsqrt(trace_value / (NRB * BLOCK_EDGE * R))).reshape(NRB, BLOCK_EDGE * R)
    gram = gmat * (R / trace_value)
    return (new_rows, gram)
```

```python
import functools
import math

import jax
import jax.numpy as jnp
from jax import lax
from jax.experimental import pallas as pl
from jax.experimental.pallas import tpu as pltpu
from jax.sharding import PartitionSpec as P

MESH = pl.DeviceIdType.MESH
F32 = jnp.float32
BF16 = jnp.bfloat16
NT = (((1,), (1,)), ((), ()))


def place_of(n):
    d = lax.axis_index("dev")
    return lax.axis_index("grp"), d // (2 * n), (d // 2) % n, d % 2


def remote(src, dst, send, recv, target):
    copy = pltpu.make_async_remote_copy(
        src_ref=src, dst_ref=dst, send_sem=send, recv_sem=recv, device_id=target, device_id_type=MESH
    )
    copy.start()
    return copy


def look_place(ids, row_place):
    table = jnp.arange(row_place.shape[0])
    hits = ids[:, None] == table[None, :]
    return jnp.sum(jnp.where(hits, row_place[None, :], 0), axis=1)


def gather_kernel(n, two, three, out2, out3, own_sem, s1, r1, s2, r2, s3, r3):
    g, z, y, c = place_of(n)

    def dev(zz, yy, cc):
        return (g, (zz * n + yy) * 2 + cc)

    sibling = dev(z, y, 1 - c)
    barrier = pltpu.get_barrier_semaphore()
    for k in range(1, n):
        pl.semaphore_signal(barrier, inc=1, device_id=dev((z + k) % n, y, c), device_id_type=MESH)
        pl.semaphore_signal(barrier, inc=1, device_id=dev(z, (y + k) % n, c), device_id_type=MESH)
    pl.semaphore_signal(barrier, inc=1, device_id=sibling, device_id_type=MESH)
    own = [
        pltpu.make_async_copy(two, out2.at[z, y, c], own_sem.at[0]),
        pltpu.make_async_copy(three, out3.at[z, y, c], own_sem.at[1]),
    ]
    for copy in own:
        copy.start()
    pl.semaphore_wait(barrier, 2 * (n - 1) + 1)

    first = []
    for k in range(1, n):
        first.append(remote(two, out2.at[z, y, c], s1.at[0, k], r1.at[0, k], dev((z + k) % n, y, c)))
        first.append(remote(three, out3.at[z, y, c], s1.at[1, k], r1.at[1, k], dev(z, (y + k) % n, c)))
    for copy in own:
        copy.wait()
    for copy in first:
        copy.wait_recv()

    half = n // 2

    def bundle(which, at, part):
        lo, size = (0, n) if part is None else (part * half, half)
        if which == 0:
            return out2.at[pl.ds(lo, size), at, c]
        return out3.at[at, pl.ds(lo, size), c]

    def neighbour(which, step):
        if which == 0:
            return dev(z, (y + step + n) % n, c)
        return dev((z + step + n) % n, y, c)

    me = (y, z)
    sends, siblings = list(first), []

    def to_sibling(which, slot, at, part):
        ref = bundle(which, at, part)
        siblings.append(remote(ref, ref, s3.at[which, slot], r3.at[which, slot], sibling))

    rings = {}

    def pass_on(which, side, k, at):
        part = None if k < half else side
        ref = bundle(which, at, part)
        copy = remote(
            ref, ref, s2.at[which, side, k], r2.at[which, side, k], neighbour(which, 1 if side == 0 else -1)
        )
        rings[which, side, k] = copy
        sends.append(copy)

    for which in (0, 1):
        for side in (0, 1):
            pass_on(which, side, 1, me[which])
    for which in (0, 1):
        to_sibling(which, 0, me[which], None)
    for k in range(1, half + 1):
        for which in (0, 1):
            for side in (0, 1):
                rings[which, side, k].wait_recv()
                at = (me[which] + (n - k if side == 0 else k)) % n
                if k + 1 <= half:
                    pass_on(which, side, k + 1, at)
                to_sibling(which, 1 + 2 * (k - 1) + side, at, None if k < half else side)
    for copy in siblings:
        copy.wait_recv()
    for copy in sends + siblings:
        copy.wait_send()


def gather_factors(n, two, three):
    shape = jax.ShapeDtypeStruct((n, n, 2) + two.shape, two.dtype)
    dma = pltpu.SemaphoreType.DMA
    vmem = pl.BlockSpec(memory_space=pltpu.VMEM)
    return pl.pallas_call(
        functools.partial(gather_kernel, n),
        out_shape=(shape, shape),
        in_specs=[vmem] * 2,
        out_specs=(vmem, vmem),
        scratch_shapes=[
            dma((2,)),
            dma((2, n)),
            dma((2, n)),
            dma((2, 2, n)),
            dma((2, 2, n)),
            dma((2, n + 1)),
            dma((2, n + 1)),
        ],
        compiler_params=pltpu.CompilerParams(collective_id=0, has_side_effects=True),
        name="gather_factors",
    )(two, three)


def halves(v, odd):
    low = lax.broadcasted_iota(jnp.int32, v.shape, 1) < 64
    turned = pltpu.roll(v, 64, 1)
    left = jnp.where(low, v, turned)
    right = jnp.where(low, turned, v)
    return jnp.where(odd == 1, right, left)


def swap_pair(v0, v1):
    low = lax.broadcasted_iota(jnp.int32, v0.shape, 1) < 64
    even = jnp.where(low, v0, pltpu.roll(v1, 64, 1))
    odd = jnp.where(low, pltpu.roll(v0, 64, 1), v1)
    return even, odd


def local_kernel(info, blk, u2, u3, f1, panel, part, gs, xs, fs, uw, g2):
    s = pl.program_id(0)
    slots = pl.num_programs(0)
    for j in range(32):
        gs[j * 64 : (j + 1) * 64, :] = blk[0, :, j * 128 : (j + 1) * 128].astype(F32)
    for q in range(32):
        v0 = gs[pl.ds(2 * q, 32, stride=64), :]
        v1 = gs[pl.ds(2 * q + 1, 32, stride=64), :]
        even, odd = swap_pair(v0, v1)
        lanes = slice((q % 2) * 128, (q % 2) * 128 + 128)
        xs[q // 2, 0:32, lanes] = even.astype(BF16)
        xs[q // 2, 32:64, lanes] = odd.astype(BF16)

    lower = halves(u3[0].astype(F32), info[1, s] % 2)
    wide = jnp.concatenate([lower, lower], axis=1)
    wide = jnp.concatenate([wide] * 4, axis=0)
    rows = lax.broadcasted_iota(jnp.int32, wide.shape, 0) // 64
    cols = lax.broadcasted_iota(jnp.int32, wide.shape, 1) // 64
    wide = jnp.where(rows == cols, wide, 0.0).astype(BF16)
    first = jnp.dot(xs[...].reshape(1024, 256), wide, preferred_element_type=F32)
    start = pl.multiple_of(s * 64, 64)
    fs[:, pl.ds(start, 64), :] = first.astype(BF16).reshape(16, 64, 256)

    upper = halves(u2[0].astype(F32), info[0, s] % 2)
    owner = lax.broadcasted_iota(jnp.int32, upper.shape, 1) // 64
    keep = jnp.logical_and(owner == info[2, s], info[3, s] == 1)
    uw[pl.ds(start, 64), :] = jnp.where(keep, upper, 0.0).astype(BF16)

    @pl.when(s == slots - 1)
    def _():
        eye = (
            lax.broadcasted_iota(jnp.int32, (128, 128), 0) == lax.broadcasted_iota(jnp.int32, (128, 128), 1)
        ).astype(BF16)
        weights = lax.dot_general(eye, uw[...], NT, preferred_element_type=F32).astype(BF16)
        for q in range(16):
            out = jnp.dot(weights, fs[q], preferred_element_type=F32)
            g2[q * 256 : q * 256 + 128, :] = out[:, 0:128]
            g2[q * 256 + 128 : q * 256 + 256, :] = out[:, 128:256]
        for q in range(32):
            pair = []
            for r in (2 * q, 2 * q + 1):
                low = g2[pl.ds(r, 32, stride=128), :]
                high = g2[pl.ds(64 + r, 32, stride=128), :]
                pair.append(jnp.concatenate([low, high], axis=0))
            even, odd = swap_pair(*pair)
            lanes = slice((q % 2) * 128, (q % 2) * 128 + 128)
            panel[q // 2, 0:64, lanes] = even.astype(BF16)
            panel[q // 2, 64:128, lanes] = odd.astype(BF16)
        for q in range(16):
            part[q] = jnp.dot(f1[...], panel[q], preferred_element_type=F32)


def local_terms(info, blocks, two, three, f1):
    slots = blocks.shape[0]
    const2, const3 = (lambda s, i: (0, 0)), (lambda s, i: (0, 0, 0))
    return pl.pallas_call(
        local_kernel,
        grid_spec=pltpu.PrefetchScalarGridSpec(
            num_scalar_prefetch=1,
            grid=(slots,),
            in_specs=[
                pl.BlockSpec((1, 64, 4096), lambda s, i: (s, 0, 0)),
                pl.BlockSpec((1, 64, 128), lambda s, i: (i[0, s] // 2, 0, 0)),
                pl.BlockSpec((1, 64, 128), lambda s, i: (i[1, s] // 2, 0, 0)),
                pl.BlockSpec((64, 128), const2),
            ],
            out_specs=(pl.BlockSpec((16, 128, 256), const3), pl.BlockSpec((16, 64, 256), const3)),
            scratch_shapes=[
                pltpu.VMEM((2048, 128), F32),
                pltpu.VMEM((16, 64, 256), BF16),
                pltpu.VMEM((16, 64 * slots, 256), BF16),
                pltpu.VMEM((64 * slots, 128), BF16),
                pltpu.VMEM((4096, 128), F32),
            ],
        ),
        out_shape=(
            jax.ShapeDtypeStruct((16, 128, 256), BF16),
            jax.ShapeDtypeStruct((16, 64, 256), F32),
        ),
        compiler_params=pltpu.CompilerParams(dimension_semantics=("arbitrary",)),
        name="local_terms",
    )(info, blocks, two, three, f1)


def tail_kernel(
    n, nx, scale, panel, part, rows_out, gram_out,
    got_a, send_b, got_b, send_c, got_c, got_d, got_e, proj, row_t, got_h, gm, got_i, sum_i, got_j, sum_j, got_k,
    sa, ra, sb, rb, sc, rc, sd, rd, se, re, sf, rf, sg, rg, sh, rh, si, ri, sj, rj, sk, rk,
):
    g, z, y, c = place_of(n)

    def dev(zz, yy, cc):
        return (g, (zz * n + yy) * 2 + cc)

    def along_z(k):
        return dev((z + k) % n, y, c)

    def along_y(k):
        return dev(z, (y + k) % n, c)

    def along_x(k):
        return ((g + k) % nx, (z * n + y) * 2 + c)

    sibling = dev(z, y, 1 - c)
    barrier = pltpu.get_barrier_semaphore()
    for k in range(1, n):
        pl.semaphore_signal(barrier, inc=1, device_id=along_z(k), device_id_type=MESH)
        pl.semaphore_signal(barrier, inc=1, device_id=along_y(k), device_id_type=MESH)
    for k in range(1, nx):
        pl.semaphore_signal(barrier, inc=1, device_id=along_x(k), device_id_type=MESH)
    pl.semaphore_signal(barrier, inc=1, device_id=sibling, device_id_type=MESH)
    pl.semaphore_wait(barrier, 2 * (n - 1) + nx)

    gp = 8 // n
    tp = 8 * gp // n
    inner = (along_z, along_y)
    outer = (along_y, along_z)
    at_in = (z, y)
    at_out = (y, z)
    sends = []

    copy = remote(part.at[pl.ds((1 - c) * 8, 8)], got_a, sa, ra, sibling)
    sends.append(copy)
    copy.wait_recv()
    for q in range(8):
        both = part[c * 8 + q] + got_a[q]
        send_b[0, q] = both[0:32].astype(BF16)
        send_b[1, q] = both[32:64].astype(BF16)

    batch = []
    for k in range(1, n):
        for st in (0, 1):
            to = (at_in[st] + k) % n
            batch.append(remote(
                send_b.at[st, pl.ds(to * gp, gp)], got_b.at[st, k], sb.at[st, k], rb.at[st, k], inner[st](k)
            ))
    for copy in batch:
        copy.wait_recv()
    sends += batch
    for st in (0, 1):
        for q in range(gp):
            at = at_in[st] * gp + q
            total = (part[c * 8 + at] + got_a[at])[st * 32 : st * 32 + 32]
            for k in range(1, n):
                total = total + got_b[st, k, q].astype(F32)
            for i in range(4):
                for h in range(2):
                    send_c[st, q * 8 + i * 2 + h] = total[i * 8 : i * 8 + 8, h * 128 : h * 128 + 128]

    batch = []
    for k in range(1, n):
        for st in (0, 1):
            to = (at_out[st] + k) % n
            batch.append(remote(
                send_c.at[st, pl.ds(to * tp, tp)], got_c.at[st, k], sc.at[st, k], rc.at[st, k], outer[st](k)
            ))
    for copy in batch:
        copy.wait_recv()
    sends += batch
    for st in (0, 1):
        total = send_c[st, pl.ds(at_out[st] * tp, tp)]
        for k in range(1, n):
            total = total + got_c[st, k]
        got_d[g, st] = total

    batch = []
    for k in range(1, nx):
        batch.append(remote(got_d.at[g], got_d.at[g], sd.at[k], rd.at[k], along_x(k)))
    for copy in batch:
        copy.wait_recv()
    sends += batch
    for st in (0, 1):
        total = got_d[0, st]
        for k in range(1, nx):
            total = total + got_d[k, st]
        got_e[st, pl.ds(at_out[st] * tp, tp)] = total

    batch = []
    for k in range(1, n):
        for st in (0, 1):
            ref = got_e.at[st, pl.ds(at_out[st] * tp, tp)]
            batch.append(remote(ref, ref, se.at[st, k], re.at[st, k], outer[st](k)))
    for copy in batch:
        copy.wait_recv()
    sends += batch
    for st in (0, 1):
        for q in range(gp):
            lines = []
            for i in range(4):
                tiles = [got_e[st, q * 8 + i * 2 + h] for h in range(2)]
                lines.append(jnp.concatenate(tiles, axis=1))
            proj[c, st, at_in[st] * gp + q] = jnp.concatenate(lines, axis=0).astype(BF16)

    batch = []
    for k in range(1, n):
        for st in (0, 1):
            ref = proj.at[c, st, pl.ds(at_in[st] * gp, gp)]
            batch.append(remote(ref, ref, sf.at[st, k], rf.at[st, k], inner[st](k)))
    for copy in batch:
        copy.wait_recv()
    sends += batch

    copy = remote(proj.at[c], proj.at[c], sg, rg, sibling)
    sends.append(copy)

    def columns(core):
        total = jnp.zeros((64, 128), F32)
        for q in range(8):
            piece = jnp.concatenate([proj[core, 0, q], proj[core, 1, q]], axis=0)
            total = total + lax.dot_general(piece, panel[core * 8 + q], NT, preferred_element_type=F32)
        return total

    mine = columns(c)
    copy.wait_recv()
    got_h[g] = mine + columns(1 - c)

    batch = []
    for k in range(1, nx):
        batch.append(remote(got_h.at[g], got_h.at[g], sh.at[k], rh.at[k], along_x(k)))
    for copy in batch:
        copy.wait_recv()
    sends += batch
    rows = got_h[0]
    for k in range(1, nx):
        rows = rows + got_h[k]
    row_t[...] = rows

    gram = lax.dot_general(rows, rows, NT, precision=lax.Precision.HIGHEST, preferred_element_type=F32)
    gm[...] = jnp.concatenate([gram[0:32], gram[32:64]], axis=1)
    copy = remote(gm, got_i, si, ri, sibling)
    copy.wait_recv()
    sends.append(copy)
    got_j[z] = gm[...] + got_i[...]
    batch = []
    for k in range(1, n):
        batch.append(remote(got_j.at[z], got_j.at[z], sj.at[k], rj.at[k], along_z(k)))
    for copy in batch:
        copy.wait_recv()
    sends += batch
    total = got_j[0]
    for k in range(1, n):
        total = total + got_j[k]
    got_k[y] = total
    batch = []
    for k in range(1, n):
        batch.append(remote(got_k.at[y], got_k.at[y], sk.at[k], rk.at[k], along_y(k)))
    for copy in batch:
        copy.wait_recv()
    sends += batch
    total = got_k[0]
    for k in range(1, n):
        total = total + got_k[k]
    gram = jnp.concatenate([total[:, 0:64], total[:, 64:128]], axis=0)
    diagonal = lax.broadcasted_iota(jnp.int32, (64, 64), 0) == lax.broadcasted_iota(jnp.int32, (64, 64), 1)
    trace = jnp.sum(jnp.where(diagonal, gram, 0.0), axis=(0, 1), keepdims=True)
    gram_out[...] = gram * (64.0 / trace)
    rows_out[...] = row_t[...] * lax.rsqrt(trace / scale)
    for copy in sends:
        copy.wait_send()


def tail(n, nx, scale, panel, part):
    dma = pltpu.SemaphoreType.DMA
    vmem = pl.BlockSpec(memory_space=pltpu.VMEM)
    gp = 8 // n
    tp = 8 * gp // n
    sems = []
    for shape in ((), (2, n), (2, n), (nx,), (2, n), (2, n), (), (nx,), (), (n,), (n,)):
        sems += [dma(shape) if shape else dma] * 2
    return pl.pallas_call(
        functools.partial(tail_kernel, n, nx, scale),
        out_shape=(jax.ShapeDtypeStruct((64, 128), F32), jax.ShapeDtypeStruct((64, 64), F32)),
        in_specs=[vmem] * 2,
        out_specs=(vmem, vmem),
        scratch_shapes=[
            pltpu.VMEM((8, 64, 256), F32),
            pltpu.VMEM((2, 8, 32, 256), BF16),
            pltpu.VMEM((2, n, gp, 32, 256), BF16),
            pltpu.VMEM((2, n * tp, 8, 128), F32),
            pltpu.VMEM((2, n, tp, 8, 128), F32),
            pltpu.VMEM((nx, 2, tp, 8, 128), F32),
            pltpu.VMEM((2, n * tp, 8, 128), F32),
            pltpu.VMEM((2, 2, 8, 32, 256), BF16),
            pltpu.VMEM((64, 128), F32),
            pltpu.VMEM((nx, 64, 128), F32),
            pltpu.VMEM((32, 128), F32),
            pltpu.VMEM((32, 128), F32),
            pltpu.VMEM((32, 128), F32),
            pltpu.VMEM((n, 32, 128), F32),
            pltpu.VMEM((32, 128), F32),
            pltpu.VMEM((n, 32, 128), F32),
        ] + sems,
        compiler_params=pltpu.CompilerParams(collective_id=1, has_side_effects=True),
        name="tail",
    )(panel, part)


def body(n, nx, blocks, coords, counts, row_place, factor_one, factor_two, factor_three):
    slots = blocks.shape[0]
    live = (jnp.arange(slots) < counts[0]).astype(jnp.int32)
    places = look_place(coords.reshape(-1), row_place).reshape(3, slots)
    info = jnp.stack([places[1], places[2], places[0] % 2, live]).astype(jnp.int32)
    two = factor_two.reshape(2, 32, 2, 64).transpose(2, 1, 0, 3).reshape(64, 128)
    three = factor_three.reshape(2, 64, 64).transpose(1, 0, 2).reshape(64, 128)
    one = factor_one.reshape(2, 32, 2, 64).transpose(3, 2, 0, 1).reshape(64, 128)
    all2, all3 = gather_factors(n, two, three)
    panel, part = local_terms(
        info, blocks, all2.reshape(-1, 64, 128), all3.reshape(-1, 64, 128), one
    )
    scale = 2.0 * 64 * 64 * 2 * n * n
    rows, gram = tail(n, nx, scale, panel, part)
    new_rows = rows.reshape(64, 2, 2, 32).transpose(2, 3, 1, 0).reshape(2, 4096)
    return (new_rows, gram)


def solution(mesh):
    n = math.isqrt(mesh.shape["dev"] // 2)
    nx = mesh.shape["grp"]
    placed = (
        P(("grp", "dev"), None, None),
        P(None, ("grp", "dev")),
        P(("grp", "dev")),
        P(),
        P("dev", None),
        P("dev", None),
        P("dev", None),
    )
    return jax.shard_map(
        functools.partial(body, n, nx), mesh=mesh, in_specs=placed, out_specs=(P("dev", None), P()), check_vma=False
    )
```
